32 devices in a mesh: ctx: 8 (over y, x, core), tp: 4 (over z).
Axes of the slice: x: 2, y: 2, z: 4, core: 2. Of those that a mesh axis runs over, the one named last changes fastest.
Arguments:
- layer_input: bfloat16 [4096, 5120], P('ctx', 'tp'), may hold values from -6 to 6
- w_query: bfloat16 [5120, 5120], P(None, 'tp'), may hold values from -0.078125 to 0.078125
- w_key: bfloat16 [5120, 1024], P(None, 'tp'), may hold values from -0.078125 to 0.078125
- w_value: bfloat16 [5120, 1024], P(None, 'tp'), may hold values from -0.078125 to 0.078125
- queries: bfloat16 [4096, 5120], P('ctx', 'tp'), may hold values from -40 to 40
- keys: bfloat16 [4096, 1024], P('ctx', 'tp'), may hold values from -4 to 4
- values: bfloat16 [4096, 1024], P('ctx', 'tp'), may hold values from -6 to 6
- grad_out: bfloat16 [4096, 5120], P('ctx', 'tp'), may hold values from -1.5 to 1.5
- block_lists: int32 [32, 6], P('ctx'), may hold values from -1 to 31, as said below
- global_ids: int32 [2], replicated, may hold values from 0 to 15, as said below
Outputs:
- grad_x: bfloat16 [4096, 5120], P('ctx', 'tp')
- grad_w_query: bfloat16 [5120, 5120], P('ctx', 'tp')
- grad_w_key: bfloat16 [5120, 1024], P('ctx', 'tp')
- grad_w_value: bfloat16 [5120, 1024], P('ctx', 'tp')
The draws below stay inside these ranges and needn't reach their ends.
Inputs may be any that keep to these rules, and one draw needn't show every extreme that they name: `global_ids`: 2 distinct blocks of the first half of the sequence; the last block of the first half is always one of them. `block_lists`: row a lists distinct key blocks b <= a that are not global, -1 for an empty slot: block a itself, a - 1 and a - 2 where they exist and are not global, then blocks drawn at random below a.
All inputs are finite; a program needn't handle non-finite values.
Results may differ from the reference program's by a relative error of at most 0.025.
Values may be sent and summed in bfloat16 or wider, within the bound.
No kernel may reach another device: no remote copies, remote signals or barrier semaphores. Data moves between devices by JAX's collectives and lax.ppermute only.
A program may use at most 192 MiB of HBM per device.

```python
import math
import jax
import jax.numpy as jnp
from jax import lax

D = 5120
H = 40
KVH = 8
HD = 128
BLK = 128
NWR = 6
NGLOB = 2
TOK_DEV = 512
TOKENS = 4096
BLOCKS = 32
N_CTX = 8


def lists_and_globals(key):
    base = jax.random.fold_in(key, 7)
    front_blocks = BLOCKS // 2
    shuffled = jax.random.permutation(jax.random.fold_in(base, 1), front_blocks - 1).astype(jnp.int32)
    chosen = jnp.concatenate([jnp.full((1,), front_blocks - 1, jnp.int32), shuffled[:NGLOB - 1]])
    row_ids = jnp.arange(BLOCKS, dtype=jnp.int32)[:, None]
    col_ids = jnp.arange(BLOCKS, dtype=jnp.int32)[None, :]
    col_global = jnp.any(col_ids[:, :, None] == chosen[None, None, :], axis=-1)
    random_rank = jax.random.randint(jax.random.fold_in(base, 2), (BLOCKS, BLOCKS), 0, BLOCKS).astype(jnp.int32)
    priority = jnp.where(col_ids >= row_ids - 2, 2 * BLOCKS * BLOCKS + col_ids, BLOCKS + random_rank * BLOCKS + col_ids)
    priority = jnp.where((col_ids > row_ids) | col_global, -1 - col_ids, priority)
    top_values, top_index = lax.top_k(priority, NWR)
    block_table = jnp.where(top_values >= 0, top_index, -1).astype(jnp.int32)
    return (block_table, chosen)


def draw_block_lists(key, part):
    return lists_and_globals(key)[0]


def draw_global_ids(key, part):
    return lists_and_globals(key)[1]


def queries_and_keys(key):
    base = jax.random.fold_in(key, 11)
    groups = H // KVH
    query_raw = jnp.clip(jax.random.normal(jax.random.fold_in(base, 1), (BLOCKS, BLK, KVH, groups, HD), jnp.float32), -4.0, 4.0)
    key_raw = jnp.clip(jax.random.normal(jax.random.fold_in(base, 2), (BLOCKS, BLK, KVH, HD), jnp.float32), -4.0, 4.0)
    return (query_raw.reshape(TOKENS, H * HD).astype(jnp.bfloat16), key_raw.reshape(TOKENS, KVH * HD).astype(jnp.bfloat16))


def draw_queries(key, part):
    return queries_and_keys(key)[0]


def draw_keys(key, part):
    return queries_and_keys(key)[1]


def with_spikes(array, rng, source, target, blocks, factor):
    def block_of(axis_at):
        return (jnp.arange(array.shape[axis_at]) // (array.shape[axis_at] // blocks)).reshape((-1,) + (1,) * (array.ndim - 1 - axis_at))

    first = jax.random.permutation(rng, blocks)[block_of(target)]
    other_side = (block_of(target) + blocks // 2) % blocks
    return jnp.where((block_of(source) == first) | (block_of(source) == other_side), factor * array, array)


def steps_of(stream_key, extent, cuts, low, top_value):
    loudness = 1.0
    for dim, parts in cuts:
        heights = jax.random.uniform(jax.random.fold_in(jax.random.fold_in(stream_key, 6), dim), (parts,), jnp.float32, low / len(cuts), top_value / len(cuts))
        loudness = loudness * jnp.repeat(jnp.exp(heights), extent[dim] // parts).reshape((-1,) + (1,) * (len(extent) - 1 - dim))
    return loudness


def gaussian(own_key, dims, deviation, most, split=(), held_as=jnp.bfloat16):
    array = deviation * jax.random.normal(own_key, dims, jnp.float32)
    if split:
        array = array * steps_of(own_key, dims, split, -0.22, 0.18)
    return jnp.clip(array, -most, most).astype(held_as)


def heavy_noise(own_key, extent, scale, limit, shards, heavy, kind=jnp.bfloat16):
    values = scale * jax.random.normal(own_key, extent, jnp.float32)
    if shards:
        values = values * steps_of(own_key, extent, shards, -0.22, 0.18)
    return jnp.clip(with_spikes(values, jax.random.fold_in(own_key, 3), *heavy), -limit, limit).astype(kind)


def setup_inputs(seed: int = 0) -> dict:
    key_list = jax.random.split(jax.random.key(seed), 11)
    layer_input = heavy_noise(key_list[0], (TOKENS, D), 1.0, 6.0, ((0, 8), (1, 4)), (0, 1, 8, 2.0))
    w_query = gaussian(key_list[1], (D, H * HD), D ** -0.5, 0.078125, ((1, 4),))
    w_key = gaussian(key_list[2], (D, KVH * HD), D ** -0.5, 0.078125, ((1, 4),))
    w_value = gaussian(key_list[3], (D, KVH * HD), D ** -0.5, 0.078125, ((1, 4),))
    queries = draw_queries(jax.random.fold_in(key_list[10], 71), 0)
    keys = draw_keys(jax.random.fold_in(key_list[10], 71), 0)
    values = gaussian(key_list[6], (TOKENS, KVH * HD), 1.0, 6.0, ((0, 8), (1, 4)))
    grad_out = gaussian(key_list[7], (TOKENS, H * HD), 0.25, 1.5, ((0, 8), (1, 4)))
    block_lists = draw_block_lists(jax.random.fold_in(key_list[10], 71), 0)
    global_ids = draw_global_ids(jax.random.fold_in(key_list[10], 71), 0)
    return {"layer_input": layer_input, "w_query": w_query, "w_key": w_key, "w_value": w_value, "queries": queries, "keys": keys, "values": values, "grad_out": grad_out, "block_lists": block_lists, "global_ids": global_ids}


masked_score = -1e+30

def row_grads(query_rows, dout_rows, key_rows, value_rows, keep_mask):
    score_scale = 1.0 / math.sqrt(query_rows.shape[-1])
    query_f = query_rows.astype(jnp.float32)
    dout_f = dout_rows.astype(jnp.float32)
    key_f = key_rows.astype(jnp.float32)
    value_f = value_rows.astype(jnp.float32)
    scores = jnp.einsum('rgd,ud->gru', query_f, key_f) * score_scale
    scores = jnp.where(keep_mask[None], scores, masked_score)
    row_top = lax.optimization_barrier(jnp.max(scores, axis=-1, keepdims=True))
    row_total = lax.optimization_barrier(jnp.sum(jnp.where(keep_mask[None], jnp.exp(scores - row_top), 0.0), axis=-1, keepdims=True))
    prob_f32 = jnp.where(keep_mask[None], jnp.exp(scores - (row_top + jnp.log(row_total))), 0.0)
    prob_b = prob_f32.astype(jnp.bfloat16).astype(jnp.float32)
    output = jnp.einsum('gru,ud->rgd', prob_b, value_f)
    delta = lax.optimization_barrier(jnp.sum(dout_f * output, axis=-1))
    dprob = jnp.einsum('rgd,ud->gru', dout_f, value_f)
    dscore = (prob_f32 * (dprob - jnp.transpose(delta)[:, :, None]) * score_scale).astype(jnp.bfloat16).astype(jnp.float32)
    query_grad = jnp.einsum('gru,ud->rgd', dscore, key_f)
    key_grad = jnp.einsum('gru,rgd->ud', dscore, query_f)
    value_grad = jnp.einsum('gru,rgd->ud', prob_b, dout_f)
    return (query_grad, key_grad, value_grad)

def reference(layer_input, w_query, w_key, w_value, queries, keys, values, grad_out, block_lists, global_ids):
    groups = H // KVH
    slot_count = NWR + NGLOB
    query_heads = queries.reshape(TOKENS, KVH, groups, HD)
    dout_heads = grad_out.reshape(TOKENS, KVH, groups, HD)
    key_heads = keys.reshape(TOKENS, KVH, HD)
    value_heads = values.reshape(TOKENS, KVH, HD)
    block_ids = jnp.arange(BLOCKS, dtype=jnp.int32)
    is_global = jnp.any(block_ids[:, None] == global_ids[None, :], axis=1)
    slot_ids = jnp.concatenate([jnp.maximum(block_lists, 0), jnp.broadcast_to(global_ids[None, :], (BLOCKS, NGLOB))], axis=1).astype(jnp.int32)
    usable = jnp.concatenate([block_lists >= 0, global_ids[None, :] <= block_ids[:, None]], axis=1) & ~is_global[:, None]
    causal = jnp.arange(BLK, dtype=jnp.int32)[None, :] <= jnp.arange(BLK, dtype=jnp.int32)[:, None]
    positions = jnp.arange(TOKENS, dtype=jnp.int32)

    def one_head(head_num):
        query_one = query_heads[:, head_num]
        dout_one = dout_heads[:, head_num]
        key_one = key_heads[:, head_num]
        value_one = value_heads[:, head_num]
        query_blk = query_one.reshape(BLOCKS, BLK, groups, HD)
        dout_blk = dout_one.reshape(BLOCKS, BLK, groups, HD)
        key_blk = key_one.reshape(BLOCKS, BLK, HD)
        value_blk = value_one.reshape(BLOCKS, BLK, HD)

        def one_block(block_num):
            chosen = slot_ids[block_num]
            allowed = usable[block_num]
            key_sel = key_blk[chosen].reshape(slot_count * BLK, HD)
            value_sel = value_blk[chosen].reshape(slot_count * BLK, HD)
            keep_mask = allowed[None, :, None] & ((chosen != block_num)[None, :, None] | causal[:, None, :])
            return row_grads(query_blk[block_num], dout_blk[block_num], key_sel, value_sel, keep_mask.reshape(BLK, slot_count * BLK))
        query_grad, key_sel_grad, value_sel_grad = lax.map(one_block, block_ids)
        flat_slots = slot_ids.reshape(-1)
        key_grad = jnp.zeros((BLOCKS, BLK, HD), jnp.float32).at[flat_slots].add(key_sel_grad.reshape(BLOCKS * slot_count, BLK, HD))
        value_grad = jnp.zeros((BLOCKS, BLK, HD), jnp.float32).at[flat_slots].add(value_sel_grad.reshape(BLOCKS * slot_count, BLK, HD))
        query_grad = query_grad.reshape(TOKENS, groups, HD)
        key_grad = key_grad.reshape(TOKENS, HD)
        value_grad = value_grad.reshape(TOKENS, HD)
        for global_num in range(NGLOB):
            row_start = (global_ids[global_num] * BLK).astype(jnp.int32)
            query_rows = lax.dynamic_slice_in_dim(query_one, row_start, BLK, 0)
            dout_rows = lax.dynamic_slice_in_dim(dout_one, row_start, BLK, 0)
            keep_mask = positions[None, :] <= row_start + jnp.arange(BLK, dtype=jnp.int32)[:, None]
            query_part, key_part, value_part = row_grads(query_rows, dout_rows, key_one, value_one, keep_mask)
            current = lax.dynamic_slice_in_dim(query_grad, row_start, BLK, 0)
            query_grad = lax.dynamic_update_slice_in_dim(query_grad, current + query_part, row_start, 0)
            key_grad = key_grad + key_part
            value_grad = value_grad + value_part
        return (query_grad, key_grad, value_grad)
    query_grad, key_grad, value_grad = lax.map(one_head, jnp.arange(KVH, dtype=jnp.int32))
    query_b = jnp.transpose(query_grad, (1, 0, 2, 3)).reshape(TOKENS, H * HD).astype(jnp.bfloat16)
    key_b = jnp.transpose(key_grad, (1, 0, 2)).reshape(TOKENS, KVH * HD).astype(jnp.bfloat16)
    value_b = jnp.transpose(value_grad, (1, 0, 2)).reshape(TOKENS, KVH * HD).astype(jnp.bfloat16)
    grad_x = jnp.dot(query_b, w_query.T, preferred_element_type=jnp.float32)
    grad_x = grad_x + jnp.dot(key_b, w_key.T, preferred_element_type=jnp.float32)
    grad_x = grad_x + jnp.dot(value_b, w_value.T, preferred_element_type=jnp.float32)

    def accumulate(totals, pieces):
        input_run = pieces[0]
        updated = []
        for total_one, grad_run in zip(totals, pieces[1:]):
            partial_b = jnp.dot(input_run.T, grad_run, preferred_element_type=jnp.float32).astype(jnp.bfloat16)
            partial_b = lax.optimization_barrier(partial_b)
            updated.append(total_one + partial_b.astype(jnp.float32))
        return (tuple(updated), None)
    runs = (layer_input.reshape(N_CTX, TOK_DEV, D), query_b.reshape(N_CTX, TOK_DEV, H * HD), key_b.reshape(N_CTX, TOK_DEV, KVH * HD), value_b.reshape(N_CTX, TOK_DEV, KVH * HD))
    start_totals = (jnp.zeros((D, H * HD), jnp.float32), jnp.zeros((D, KVH * HD), jnp.float32), jnp.zeros((D, KVH * HD), jnp.float32))
    totals, unused = lax.scan(accumulate, start_totals, runs)
    return (grad_x.astype(jnp.bfloat16), totals[0].astype(jnp.bfloat16), totals[1].astype(jnp.bfloat16), totals[2].astype(jnp.bfloat16))
```

```python
import functools
import math

import jax
import jax.numpy as jnp
from jax import lax
from jax.experimental import pallas as pl
from jax.experimental.pallas import tpu as pltpu
from jax.sharding import PartitionSpec as P

H = 40
KVH = 8
HD = 128
BLK = 128
NGLOB = 2
GROUPS = H // KVH
ROWS = GROUPS * BLK
SCALE = 1.0 / math.sqrt(HD)
EXP_SCALE = SCALE * math.log2(math.e)
MASKED = -1e30
BF16 = jnp.bfloat16
F32 = jnp.float32
MIB = 1024 * 1024


def fold_rows(x):
    return x.reshape(x.shape[0] // 8, 8, x.shape[1])


def attn_kernel(places, tok_rows, lists, globs, here, q_ref, do_ref, *refs):
    pieces, refs = refs[: len(places)], refs[len(places) :]
    dq_ref, same_ref, other_ref, kv_ref, s_ref, dp_ref, dqt_ref, dk_acc, dv_acc, ids = refs
    step = pl.program_id(0)
    me = here[0]
    ctx_size = kv_ref.shape[0] // tok_rows

    @pl.when(step == 0)
    def _():
        dk_acc[...] = jnp.zeros_like(dk_acc)
        dv_acc[...] = jnp.zeros_like(dv_acc)
        for (mask, offset), piece in zip(places, pieces):
            start = pl.multiple_of((me ^ mask) * tok_rows + offset, BLK)
            kv_ref[pl.ds(start, piece.shape[0]), :] = piece[...]

    blk = me * (tok_rows // BLK) + step
    is_global = globs[0] == blk
    for g in range(1, NGLOB):
        is_global = is_global | (globs[g] == blk)

    def all_before():
        def put(i, carry):
            ids[2 + i] = i
            return carry

        lax.fori_loop(0, blk, put, 0)
        return blk

    def listed():
        count = jnp.int32(0)
        for slot in range(lists.shape[1]):
            other = lists[step, slot]
            ids[2 + count] = jnp.maximum(other, 0)
            count = count + jnp.where((other >= 0) & (other != blk), 1, 0)
        for g in range(NGLOB):
            other = globs[g]
            ids[2 + count] = other
            count = count + jnp.where(other <= blk, 1, 0)
        return count

    count = lax.cond(is_global, all_before, listed)
    odd = lax.rem(count, 2) == 1
    last = ids[1 + count]
    ids[0] = blk
    ids[1] = jnp.where(odd, last, blk)
    pairs = 1 + lax.div(count, 2)

    def stacked(ref):
        return jnp.concatenate([ref[:, g * HD : (g + 1) * HD] for g in range(GROUPS)], axis=0)

    q_rows = stacked(q_ref)
    do_rows = stacked(do_ref)
    q_cols = q_rows.T
    do_cols = do_rows.T

    def start_of(i):
        return pl.multiple_of(ids[i] * BLK, BLK)

    def pair_rows(p, half):
        cols = slice(half * HD, (half + 1) * HD)
        return jnp.concatenate(
            [kv_ref[pl.ds(start_of(2 * p), BLK), cols], kv_ref[pl.ds(start_of(2 * p + 1), BLK), cols]],
            axis=0,
        )

    def at(p):
        return pl.ds(pl.multiple_of(p * 2 * BLK, 2 * BLK), 2 * BLK)

    def scores_of(p):
        return jnp.dot(pair_rows(p, 0), q_cols, preferred_element_type=F32)

    key_pos = lax.broadcasted_iota(jnp.int32, (2 * BLK, ROWS), 0)
    query_pos = lax.broadcasted_iota(jnp.int32, (2 * BLK, ROWS), 1) & (BLK - 1)
    limit = jnp.where(odd, 2 * BLK, 0)
    keep = key_pos <= jnp.where(key_pos < BLK, query_pos, limit - 1)
    scores = jnp.where(keep, scores_of(0), MASKED)
    s_ref[at(0), :] = scores
    top8 = jnp.max(fold_rows(scores), axis=0)

    def score_pass(p, top8):
        scores = scores_of(p)
        s_ref[at(p), :] = scores
        return jnp.maximum(top8, jnp.max(fold_rows(scores), axis=0))

    top8 = lax.fori_loop(1, pairs, score_pass, top8)
    top = jnp.max(top8, axis=0, keepdims=True)

    def sum_pass(p, carry):
        total8, dot8 = carry
        e = jnp.exp2((s_ref[at(p), :] - top) * EXP_SCALE)
        dp = jnp.dot(pair_rows(p, 1), do_cols, preferred_element_type=F32)
        s_ref[at(p), :] = e
        dp_ref[at(p), :] = dp
        return (
            total8 + jnp.sum(fold_rows(e), axis=0),
            dot8 + jnp.sum(fold_rows(e * dp), axis=0),
        )

    zero8 = jnp.zeros((8, ROWS), F32)
    total8, dot8 = lax.fori_loop(0, pairs, sum_pass, (zero8, zero8))
    inverse = 1.0 / jnp.sum(total8, axis=0, keepdims=True)
    delta = jnp.sum(dot8, axis=0, keepdims=True) * inverse
    dqt_ref[...] = jnp.zeros_like(dqt_ref)

    def grad_pass(p, carry):
        prob = s_ref[at(p), :] * inverse
        ds = (prob * (dp_ref[at(p), :] - delta)).astype(BF16)
        dv = jnp.dot(prob.astype(BF16), do_rows, preferred_element_type=F32)
        dk = jnp.dot(ds, q_rows, preferred_element_type=F32)
        dqt_ref[...] += jnp.dot(pair_rows(p, 0).T, ds, preferred_element_type=F32)
        for half in range(2):
            rows = pl.ds(start_of(2 * p + half), BLK)
            part = slice(half * BLK, (half + 1) * BLK)
            dk_acc[rows, :] += dk[part]
            dv_acc[rows, :] += dv[part]
        return carry

    lax.fori_loop(0, pairs, grad_pass, 0)
    dq = (dqt_ref[...] * SCALE).T.astype(BF16)
    for g in range(GROUPS):
        dq_ref[:, g * HD : (g + 1) * HD] = dq[g * BLK : (g + 1) * BLK]

    @pl.when(step == pl.num_programs(0) - 1)
    def _():
        for chip in range(ctx_size // 2):
            out = slice(chip * tok_rows, (chip + 1) * tok_rows)
            for ref, core in ((same_ref, 0), (other_ref, 1)):
                start = pl.multiple_of((me ^ (2 * chip + core)) * tok_rows, BLK)
                rows = pl.ds(start, tok_rows)
                ref[out, :HD] = (dk_acc[rows, :] * SCALE).astype(BF16)
                ref[out, HD:] = dv_acc[rows, :].astype(BF16)


def attention_grads(head, block_lists, global_ids, here, queries, grad_out, places, pieces):
    tok_rows = queries.shape[0]
    blk_count = tok_rows // BLK
    total_rows = sum(piece.shape[0] for piece in pieces)
    slots = max(block_lists.shape[1] + NGLOB + 2, total_rows // BLK // 2 + 2)
    slots += slots % 2
    smem = pl.BlockSpec(memory_space=pltpu.SMEM)
    pair_cols = 2 * HD
    work = blk_count * 9 * BLK * ROWS
    half = pl.BlockSpec((total_rows // 2, pair_cols), lambda a: (0, 0))
    half_shape = jax.ShapeDtypeStruct((total_rows // 2, pair_cols), BF16)
    return pl.pallas_call(
        functools.partial(attn_kernel, places, tok_rows),
        grid=(blk_count,),
        in_specs=[
            smem,
            smem,
            smem,
            pl.BlockSpec((BLK, ROWS), lambda a: (a, head)),
            pl.BlockSpec((BLK, ROWS), lambda a: (a, head)),
        ]
        + [
            pl.BlockSpec(
                (piece.shape[0], pair_cols), lambda a: (0, head), pipeline_mode=pl.Buffered(1)
            )
            for piece in pieces
        ],
        out_specs=[pl.BlockSpec((BLK, ROWS), lambda a: (a, 0)), half, half],
        out_shape=[jax.ShapeDtypeStruct((tok_rows, ROWS), BF16), half_shape, half_shape],
        scratch_shapes=[
            pltpu.VMEM((total_rows, pair_cols), BF16),
            pltpu.VMEM((slots * BLK, ROWS), F32),
            pltpu.VMEM((slots * BLK, ROWS), F32),
            pltpu.VMEM((HD, ROWS), F32),
            pltpu.VMEM((total_rows, HD), F32),
            pltpu.VMEM((total_rows, HD), F32),
            pltpu.SMEM((slots + 4,), jnp.int32),
        ],
        compiler_params=pltpu.CompilerParams(
            dimension_semantics=("arbitrary",), vmem_limit_bytes=58 * MIB
        ),
        cost_estimate=pl.CostEstimate(
            flops=10 * work * HD,
            transcendentals=work,
            bytes_accessed=4 * total_rows * pair_cols + 6 * tok_rows * ROWS,
        ),
        name="attn_grads",
    )(block_lists, global_ids, here, queries, grad_out, *pieces)


def input_grad_kernel(heads, *refs):
    dq, dkv = refs[:heads], refs[heads : 2 * heads]
    wq_ref, wk_ref, wv_ref, out_ref, dk_ref, dv_ref = refs[2 * heads :]

    @pl.when(pl.program_id(0) == 0)
    def _():
        for j in range(heads):
            cols = slice(j * HD, (j + 1) * HD)
            dk_ref[:, cols] = dkv[j][:, :HD]
            dv_ref[:, cols] = dkv[j][:, HD:]

    def term(grad, weight):
        return lax.dot_general(
            grad, weight, (((1,), (1,)), ((), ())), preferred_element_type=F32
        )

    total = term(dk_ref[...], wk_ref[...]) + term(dv_ref[...], wv_ref[...])
    for j in range(heads):
        total += term(dq[j][...], wq_ref[:, j * ROWS : (j + 1) * ROWS])
    out_ref[...] = total.astype(BF16)


def input_grad(dq, dkv, w_query, w_key, w_value):
    heads = len(dq)
    rows, width = dq[0].shape[0], w_query.shape[0]
    tile = 512
    whole = [pl.BlockSpec(x.shape, lambda i: (0, 0)) for x in dq + dkv]
    cols = w_query.shape[1] + w_key.shape[1] + w_value.shape[1]
    return pl.pallas_call(
        functools.partial(input_grad_kernel, heads),
        grid=(width // tile,),
        in_specs=whole
        + [pl.BlockSpec((tile, w.shape[1]), lambda i: (i, 0)) for w in (w_query, w_key, w_value)],
        out_specs=pl.BlockSpec((rows, tile), lambda i: (0, i)),
        out_shape=jax.ShapeDtypeStruct((rows, width), BF16),
        scratch_shapes=[pltpu.VMEM((rows, heads * HD), BF16)] * 2,
        compiler_params=pltpu.CompilerParams(
            dimension_semantics=("arbitrary",), vmem_limit_bytes=40 * MIB
        ),
        cost_estimate=pl.CostEstimate(
            flops=2 * rows * width * cols,
            transcendentals=0,
            bytes_accessed=2 * (width * cols + rows * cols + rows * width),
        ),
        name="input_grad",
    )(*dq, *dkv, w_query, w_key, w_value)


def weight_grad_kernel(count, chip, x_ref, *refs):
    out_ref = refs[-1]
    own, partner = refs[:count], refs[count : 2 * count]
    inputs = x_ref[0].T
    rows = own[0].shape[0]
    start = 0
    for mine, theirs in zip(own, partner):
        total = jnp.dot(inputs[:, :rows], mine[...], preferred_element_type=F32)
        total += jnp.dot(inputs[:, rows:], theirs[...], preferred_element_type=F32)
        cols = mine.shape[1]
        out_ref[0, :, start : start + cols] = total.astype(BF16)
        start += cols


def weight_grad(chip, inputs, own, partner):
    chips, rows, width = inputs.shape
    cols = sum(x.shape[1] for x in own)
    return pl.pallas_call(
        functools.partial(weight_grad_kernel, len(own)),
        grid_spec=pltpu.PrefetchScalarGridSpec(
            num_scalar_prefetch=1,
            grid=(chips,),
            in_specs=[pl.BlockSpec((1, rows, width), lambda i, chip: (chip[0] ^ i, 0, 0))]
            + [pl.BlockSpec(x.shape, lambda i, chip: (0, 0)) for x in own + partner],
            out_specs=pl.BlockSpec((1, width, cols), lambda i, chip: (i, 0, 0)),
        ),
        out_shape=jax.ShapeDtypeStruct((chips, width, cols), BF16),
        compiler_params=pltpu.CompilerParams(
            dimension_semantics=("arbitrary",), vmem_limit_bytes=40 * MIB
        ),
        cost_estimate=pl.CostEstimate(
            flops=2 * chips * rows * width * cols,
            transcendentals=0,
            bytes_accessed=2 * (chips * width * (rows + cols) + rows * cols),
        ),
        name="weight_grad",
    )(chip, inputs, *own, *partner)


def swap(x, mask):
    return lax.ppermute(x, "ctx", [(i, i ^ mask) for i in range(lax.axis_size("ctx"))])


def gather_pieces(x):
    rows = x.shape[0]
    chips = lax.axis_size("ctx") // 2
    found = [((0, 0), x)]
    if chips == 4:
        side, front = swap(x, 2), swap(x, 4)
        half = rows // 2
        found += [((2, 0), side), ((4, 0), front)]
        found += [((6, 0), swap(front[:half], 2)), ((6, half), swap(side[half:], 4))]
    else:
        found += [((2 * i, 0), swap(x, 2 * i)) for i in range(1, chips)]
    found += [((mask ^ 1, offset), swap(piece, 1)) for (mask, offset), piece in found]
    return [place for place, _ in found], [piece for _, piece in found]


def total_of(parts):
    total = parts[0].astype(F32)
    for part in parts[1:]:
        total = total + part.astype(F32)
    return total.astype(BF16)


def shards(
    layer_input, w_query, w_key, w_value, queries, keys, values, grad_out, block_lists, global_ids
):
    tok_rows, width = layer_input.shape
    kv_heads = keys.shape[1] // HD
    chips = lax.axis_size("ctx") // 2
    here = lax.axis_index("ctx").astype(jnp.int32)
    core = here % 2
    chip = (here // 2).reshape(1)

    kv_own = jnp.concatenate(
        [
            x[:, j * HD : (j + 1) * HD]
            for j in range(kv_heads)
            for x in (keys, values)
        ],
        axis=1,
    )
    places, pieces = gather_pieces(kv_own)

    half = width // 2
    kept = lax.dynamic_slice_in_dim(layer_input, core * half, half, 1)
    given = lax.dynamic_slice_in_dim(layer_input, (1 - core) * half, half, 1)
    input_pair = jnp.concatenate([kept, swap(given, 1)], axis=0)
    runs = 2
    step = half // runs
    inputs = [
        lax.all_gather(input_pair[:, r * step : (r + 1) * step], "tp", axis=0, tiled=False)
        for r in range(runs)
    ]

    dq, dkv = [], []
    for j in range(kv_heads):
        dq_j, same, other = attention_grads(
            j, block_lists, global_ids, here.reshape(1), queries, grad_out, places, pieces
        )
        dq.append(dq_j)
        chip_sum = total_of([same, swap(other, 1)]).reshape(chips, tok_rows, 2 * HD)
        dkv.append(total_of([chip_sum[0]] + [swap(chip_sum[i], 2 * i) for i in range(1, chips)]))
    dq_partner = [swap(x, 1) for x in dq]
    dkv_partner = [swap(x, 1) for x in dkv]

    grad_x = lax.psum_scatter(
        input_grad(dq, dkv, w_query, w_key, w_value), "tp", scatter_dimension=1, tiled=True
    )

    def scattered(partial):
        return total_of([partial[0]] + [swap(partial[i], 2 * i) for i in range(1, chips)])

    grad_w_query = jnp.concatenate(
        [scattered(weight_grad(chip, x, dq, dq_partner)) for x in inputs], axis=0
    )
    grad_w_kv = jnp.concatenate(
        [scattered(weight_grad(chip, x, dkv, dkv_partner)) for x in inputs], axis=0
    )

    def columns(first):
        return jnp.concatenate(
            [grad_w_kv[:, c : c + HD] for c in range(first, 2 * HD * kv_heads, 2 * HD)], axis=1
        )

    return (grad_x, grad_w_query, columns(0), columns(HD))


def solution(mesh):
    return jax.shard_map(
        shards,
        mesh=mesh,
        in_specs=(
            P("ctx", "tp"),
            P(None, "tp"),
            P(None, "tp"),
            P(None, "tp"),
            P("ctx", "tp"),
            P("ctx", "tp"),
            P("ctx", "tp"),
            P("ctx", "tp"),
            P("ctx", None),
            P(),
        ),
        out_specs=(P("ctx", "tp"), P("ctx", "tp"), P("ctx", "tp"), P("ctx", "tp")),
        check_vma=False,
    )
```

```python
import functools
import math

import jax
import jax.numpy as jnp
from jax import lax
from jax.experimental import pallas as pl
from jax.experimental.pallas import tpu as pltpu
from jax.sharding import PartitionSpec as P

H = 40
KVH = 8
HD = 128
BLK = 128
NGLOB = 2
GROUPS = H // KVH
ROWS = GROUPS * BLK
TURN = 8
SPAN = TURN * BLK
SCALE = 1.0 / math.sqrt(HD)
EXP_SCALE = SCALE * math.log2(math.e)
MASKED = -1e30
BF16 = jnp.bfloat16
F32 = jnp.float32
MIB = 1024 * 1024


def fold_rows(x):
    return x.reshape(x.shape[0] // 8, 8, x.shape[1])


def attn_kernel(places, tok_rows, lists, globs, here, q_ref, do_ref, *refs):
    pieces, refs = refs[: len(places)], refs[len(places) :]
    dq_ref, same_ref, other_ref, kv_ref, s_ref, dp_ref, dqt_ref, dk_acc, dv_acc, ids = refs
    step = pl.program_id(0)
    me = here[0]
    ctx_size = kv_ref.shape[0] // tok_rows

    @pl.when(step == 0)
    def _():
        dk_acc[...] = jnp.zeros_like(dk_acc)
        dv_acc[...] = jnp.zeros_like(dv_acc)
        for mask, piece in zip(places, pieces):
            start = pl.multiple_of((me ^ mask) * tok_rows, BLK)
            kv_ref[pl.ds(start, piece.shape[0]), :] = piece[...]

    blk = me * (tok_rows // BLK) + step
    is_global = globs[0] == blk
    for g in range(1, NGLOB):
        is_global = is_global | (globs[g] == blk)

    def all_before():
        def put(i, carry):
            ids[TURN + i] = i
            return carry

        lax.fori_loop(0, blk, put, 0)
        return blk

    def listed():
        count = jnp.int32(0)
        for slot in range(lists.shape[1]):
            other = lists[step, slot]
            ids[TURN + count] = jnp.maximum(other, 0)
            count = count + jnp.where((other >= 0) & (other != blk), 1, 0)
        for g in range(NGLOB):
            other = globs[g]
            ids[TURN + count] = other
            count = count + jnp.where(other <= blk, 1, 0)
        return count

    count = lax.cond(is_global, all_before, listed)
    extra = lax.rem(count, TURN)
    ids[0] = blk
    for i in range(1, TURN):
        ids[i] = jnp.where(i <= extra, ids[jnp.maximum(TURN + count - i, 0)], blk)
    turns = 1 + lax.div(count, TURN)

    def stacked(ref):
        return jnp.concatenate([ref[:, g * HD : (g + 1) * HD] for g in range(GROUPS)], axis=0)

    q_rows = stacked(q_ref)
    do_rows = stacked(do_ref)
    q_cols = q_rows.T
    do_cols = do_rows.T

    def start_of(i):
        return pl.multiple_of(ids[i] * BLK, BLK)

    def keys_of(p, half):
        cols = slice(half * HD, (half + 1) * HD)
        return jnp.concatenate(
            [kv_ref[pl.ds(start_of(TURN * p + i), BLK), cols] for i in range(TURN)], axis=0
        )

    def at(p):
        return pl.ds(pl.multiple_of(p * SPAN, SPAN), SPAN)

    def scores_of(p):
        return jnp.dot(keys_of(p, 0), q_cols, preferred_element_type=F32)

    key_pos = lax.broadcasted_iota(jnp.int32, (BLK, ROWS), 0)
    query_pos = lax.broadcasted_iota(jnp.int32, (BLK, ROWS), 1) & (BLK - 1)
    scores = scores_of(0)
    parts = [jnp.where(key_pos <= query_pos, scores[:BLK], MASKED)]
    for i in range(1, TURN):
        bias = jnp.where(i <= extra, 0.0, MASKED).astype(F32)
        parts.append(scores[i * BLK : (i + 1) * BLK] + bias)
    scores = jnp.concatenate(parts, axis=0)
    s_ref[at(0), :] = scores
    top8 = jnp.max(fold_rows(scores), axis=0)

    def score_pass(p, top8):
        scores = scores_of(p)
        s_ref[at(p), :] = scores
        return jnp.maximum(top8, jnp.max(fold_rows(scores), axis=0))

    top8 = lax.fori_loop(1, turns, score_pass, top8)
    top = jnp.max(top8, axis=0, keepdims=True)

    def sum_pass(p, carry):
        total8, dot8 = carry
        e = jnp.exp2((s_ref[at(p), :] - top) * EXP_SCALE)
        dp = jnp.dot(keys_of(p, 1), do_cols, preferred_element_type=F32)
        s_ref[at(p), :] = e
        dp_ref[at(p), :] = dp
        return (
            total8 + jnp.sum(fold_rows(e), axis=0),
            dot8 + jnp.sum(fold_rows(e * dp), axis=0),
        )

    zero8 = jnp.zeros((8, ROWS), F32)
    total8, dot8 = lax.fori_loop(0, turns, sum_pass, (zero8, zero8))
    inverse = 1.0 / jnp.sum(total8, axis=0, keepdims=True)
    delta = jnp.sum(dot8, axis=0, keepdims=True) * inverse
    dqt_ref[...] = jnp.zeros_like(dqt_ref)

    def grad_pass(p, carry):
        prob = s_ref[at(p), :] * inverse
        ds = (prob * (dp_ref[at(p), :] - delta)).astype(BF16)
        dv = jnp.dot(prob.astype(BF16), do_rows, preferred_element_type=F32)
        dk = jnp.dot(ds, q_rows, preferred_element_type=F32)
        dqt_ref[...] += jnp.dot(keys_of(p, 0).T, ds, preferred_element_type=F32)
        for i in range(TURN):
            rows = pl.ds(start_of(TURN * p + i), BLK)
            part = slice(i * BLK, (i + 1) * BLK)
            dk_acc[rows, :] += dk[part]
            dv_acc[rows, :] += dv[part]
        return carry

    lax.fori_loop(0, turns, grad_pass, 0)
    dq = (dqt_ref[...] * SCALE).T.astype(BF16)
    for g in range(GROUPS):
        dq_ref[:, g * HD : (g + 1) * HD] = dq[g * BLK : (g + 1) * BLK]

    @pl.when(step == pl.num_programs(0) - 1)
    def _():
        for chip in range(ctx_size // 2):
            out = slice(chip * tok_rows, (chip + 1) * tok_rows)
            for ref, core in ((same_ref, 0), (other_ref, 1)):
                start = pl.multiple_of((me ^ (2 * chip + core)) * tok_rows, BLK)
                rows = pl.ds(start, tok_rows)
                ref[out, :HD] = (dk_acc[rows, :] * SCALE).astype(BF16)
                ref[out, HD:] = dv_acc[rows, :].astype(BF16)


def attention_grads(head, block_lists, global_ids, here, queries, grad_out, places, pieces):
    tok_rows = queries.shape[0]
    blk_count = tok_rows // BLK
    total_rows = sum(piece.shape[0] for piece in pieces)
    slots = max(block_lists.shape[1] + NGLOB + 1, total_rows // BLK // 2)
    slots = -(-slots // TURN) * TURN
    smem = pl.BlockSpec(memory_space=pltpu.SMEM)
    pair_cols = 2 * HD
    work = blk_count * 9 * BLK * ROWS
    half = pl.BlockSpec((total_rows // 2, pair_cols), lambda a: (0, 0))
    half_shape = jax.ShapeDtypeStruct((total_rows // 2, pair_cols), BF16)
    return pl.pallas_call(
        functools.partial(attn_kernel, places, tok_rows),
        grid=(blk_count,),
        in_specs=[
            smem,
            smem,
            smem,
            pl.BlockSpec((BLK, ROWS), lambda a: (a, head)),
            pl.BlockSpec((BLK, ROWS), lambda a: (a, head)),
        ]
        + [
            pl.BlockSpec(piece.shape, lambda a: (0, 0), pipeline_mode=pl.Buffered(1))
            for piece in pieces
        ],
        out_specs=[pl.BlockSpec((BLK, ROWS), lambda a: (a, 0)), half, half],
        out_shape=[jax.ShapeDtypeStruct((tok_rows, ROWS), BF16), half_shape, half_shape],
        scratch_shapes=[
            pltpu.VMEM((total_rows, pair_cols), BF16),
            pltpu.VMEM((slots * BLK, ROWS), F32),
            pltpu.VMEM((slots * BLK, ROWS), F32),
            pltpu.VMEM((HD, ROWS), F32),
            pltpu.VMEM((total_rows, HD), F32),
            pltpu.VMEM((total_rows, HD), F32),
            pltpu.SMEM((slots + TURN + 1,), jnp.int32),
        ],
        compiler_params=pltpu.CompilerParams(
            dimension_semantics=("arbitrary",), vmem_limit_bytes=58 * MIB
        ),
        cost_estimate=pl.CostEstimate(flops=1000, transcendentals=0, bytes_accessed=1000),
        name="attn_grads",
    )(block_lists, global_ids, here, queries, grad_out, *pieces)


def dot_t(rows, weight):
    return lax.dot_general(rows, weight, (((1,), (1,)), ((), ())), preferred_element_type=F32)


def query_term_kernel(heads, *refs):
    dq, (wq_ref, out_ref) = refs[:heads], refs[heads:]
    total = dot_t(dq[0][...], wq_ref[:, :ROWS])
    for j in range(1, heads):
        total += dot_t(dq[j][...], wq_ref[:, j * ROWS : (j + 1) * ROWS])
    out_ref[...] = total.astype(BF16)


def query_term(dq, w_query):
    rows, (width, cols) = dq[0].shape[0], w_query.shape
    tile = width // 4
    return pl.pallas_call(
        functools.partial(query_term_kernel, len(dq)),
        grid=(width // tile,),
        in_specs=[pl.BlockSpec(x.shape, lambda i: (0, 0)) for x in dq]
        + [pl.BlockSpec((tile, cols), lambda i: (i, 0))],
        out_specs=pl.BlockSpec((rows, tile), lambda i: (0, i)),
        out_shape=jax.ShapeDtypeStruct((rows, width), BF16),
        compiler_params=pltpu.CompilerParams(
            dimension_semantics=("arbitrary",), vmem_limit_bytes=58 * MIB
        ),
        cost_estimate=pl.CostEstimate(flops=1000, transcendentals=0, bytes_accessed=1000),
        name="query_term",
    )(*dq, w_query)


def kv_term_kernel(heads, *refs):
    grads, (base_ref, wk_ref, wv_ref, out_ref, dk_ref, dv_ref) = refs[:heads], refs[heads:]

    @pl.when(pl.program_id(0) == 0)
    def _():
        for j in range(heads):
            cols = slice(j * HD, (j + 1) * HD)
            dk_ref[:, cols] = grads[j][:, :HD]
            dv_ref[:, cols] = grads[j][:, HD:]

    total = base_ref[...].astype(F32) + dot_t(dk_ref[...], wk_ref[...]) + dot_t(dv_ref[...], wv_ref[...])
    out_ref[...] = total.astype(BF16)


def with_kv_term(base, dkv, w_key, w_value):
    rows, width = base.shape
    cols = w_key.shape[1]
    tile = width // 4
    weight = pl.BlockSpec((tile, cols), lambda i: (i, 0))
    return pl.pallas_call(
        functools.partial(kv_term_kernel, len(dkv)),
        grid=(width // tile,),
        in_specs=[pl.BlockSpec(x.shape, lambda i: (0, 0)) for x in dkv]
        + [pl.BlockSpec((rows, tile), lambda i: (0, i)), weight, weight],
        out_specs=pl.BlockSpec((rows, tile), lambda i: (0, i)),
        out_shape=jax.ShapeDtypeStruct((rows, width), BF16),
        scratch_shapes=[pltpu.VMEM((rows, cols), BF16)] * 2,
        compiler_params=pltpu.CompilerParams(
            dimension_semantics=("arbitrary",), vmem_limit_bytes=58 * MIB
        ),
        cost_estimate=pl.CostEstimate(flops=1000, transcendentals=0, bytes_accessed=1000),
        name="kv_term",
    )(*dkv, base, w_key, w_value)


def weight_grad_kernel(count, chip, x_ref, *refs):
    out_ref = refs[-1]
    own, partner = refs[:count], refs[count : 2 * count]
    inputs = x_ref[0].T
    rows = own[0].shape[0]
    start = 0
    for mine, theirs in zip(own, partner):
        total = jnp.dot(inputs[:, :rows], mine[...], preferred_element_type=F32)
        total += jnp.dot(inputs[:, rows:], theirs[...], preferred_element_type=F32)
        cols = mine.shape[1]
        out_ref[0, :, start : start + cols] = total.astype(BF16)
        start += cols


def weight_grad(chip, inputs, own, partner):
    chips, rows, width = inputs.shape
    cols = sum(x.shape[1] for x in own)
    return pl.pallas_call(
        functools.partial(weight_grad_kernel, len(own)),
        grid_spec=pltpu.PrefetchScalarGridSpec(
            num_scalar_prefetch=1,
            grid=(chips,),
            in_specs=[pl.BlockSpec((1, rows, width), lambda i, chip: (chip[0] ^ i, 0, 0))]
            + [pl.BlockSpec(x.shape, lambda i, chip: (0, 0)) for x in own + partner],
            out_specs=pl.BlockSpec((1, width, cols), lambda i, chip: (i, 0, 0)),
        ),
        out_shape=jax.ShapeDtypeStruct((chips, width, cols), BF16),
        compiler_params=pltpu.CompilerParams(
            dimension_semantics=("arbitrary",), vmem_limit_bytes=58 * MIB
        ),
        cost_estimate=pl.CostEstimate(flops=1000, transcendentals=0, bytes_accessed=1000),
        name="weight_grad",
    )(chip, inputs, *own, *partner)


def swap(x, mask):
    return lax.ppermute(x, "ctx", [(i, i ^ mask) for i in range(lax.axis_size("ctx"))])


def gather_pieces(x):
    size = lax.axis_size("ctx")
    found = [(0, x)] + [(mask, swap(x, mask)) for mask in range(2, size, 2)]
    return found + [(mask ^ 1, swap(piece, 1)) for mask, piece in found]


def after(x, *others):
    return lax.optimization_barrier((x, others))[0]


def total_of(parts):
    total = parts[0].astype(F32)
    for part in parts[1:]:
        total = total + part.astype(F32)
    return total.astype(BF16)


def scattered(partial):
    chips, rows, _ = partial.shape
    if chips != 4:
        top = total_of([partial[0]] + [swap(partial[i], 2 * i) for i in range(1, chips)])
        return [top]
    half = rows // 2
    by_side, by_front = swap(partial[3, :half], 2), swap(partial[3, half:], 4)
    side_top, front_low = swap(partial[1, :half], 2), swap(partial[2, half:], 4)
    front_top = swap(total_of([partial[2, :half], by_side]), 4)
    side_low = swap(total_of([partial[1, half:], by_front]), 2)
    return [
        total_of([partial[0, :half], side_top, front_top]),
        total_of([partial[0, half:], side_low, front_low]),
    ]


def shards(
    layer_input, w_query, w_key, w_value, queries, keys, values, grad_out, block_lists, global_ids
):
    tok_rows, width = layer_input.shape
    kv_heads = keys.shape[1] // HD
    chips = lax.axis_size("ctx") // 2
    here = lax.axis_index("ctx").astype(jnp.int32)
    core = here % 2
    chip = (here // 2).reshape(1)

    def own_kv(j):
        cols = slice(j * HD, (j + 1) * HD)
        return jnp.concatenate([keys[:, cols], values[:, cols]], axis=1)

    size = lax.axis_size("ctx")
    gathered = [gather_pieces(own_kv(0))]
    arrived = [piece for _, piece in gathered[0]]
    for j in range(1, kv_heads):
        own = after(own_kv(j), *arrived)
        gathered.append([(0, own)] + [(mask, swap(own, mask)) for mask in range(2, size, 2)])

    half = width // 2
    kept = lax.dynamic_slice_in_dim(layer_input, core * half, half, 1)
    given = lax.dynamic_slice_in_dim(layer_input, (1 - core) * half, half, 1)
    input_pair = jnp.concatenate([kept, swap(given, 1)], axis=0)
    inputs = lax.all_gather(input_pair, "tp", axis=0, tiled=False)

    dq, dkv = [], []
    ready = ()
    for j in range(kv_heads):
        dq_j, same, other = attention_grads(
            j,
            block_lists,
            global_ids,
            after(here.reshape(1), *ready),
            queries,
            grad_out,
            [mask for mask, _ in gathered[j]],
            [piece for _, piece in gathered[j]],
        )
        dq.append(dq_j)
        if j + 1 < kv_heads:
            early = [(mask, after(piece, dq_j)) for mask, piece in gathered[j + 1]]
            other = after(other, *[piece for _, piece in early])
            gathered[j + 1] = early + [(mask ^ 1, swap(piece, 1)) for mask, piece in early]
        other = after(other, *dkv)
        chip_sum = total_of([same, swap(other, 1)]).reshape(chips, tok_rows, 2 * HD)
        ready = (chip_sum,)
        if j == kv_heads - 1:
            dq_partner = [swap(x, 1) for x in dq]
            base = query_term(
                [after(dq[0], chip_sum, *dq_partner)] + dq[1:], w_query
            )
            chip_sum_last = after(chip_sum[0], base)
        else:
            chip_sum_last = after(chip_sum[0], *dq)
        dkv.append(
            total_of([chip_sum_last] + [swap(chip_sum[i], 2 * i) for i in range(1, chips)])
        )
    input_term = with_kv_term(base, dkv, w_key, w_value)
    grad_x = lax.psum_scatter(input_term, "tp", scatter_dimension=1, tiled=True)
    dkv_partner = [swap(x, 1) for x in dkv]

    part_query = weight_grad(
        chip, after(inputs, input_term), dq, dq_partner
    )
    part_kv = weight_grad(chip, inputs, [after(dkv[0], part_query)] + dkv[1:], dkv_partner)
    grad_w_query = jnp.concatenate(scattered(part_query), axis=0)
    grad_w_kv = jnp.concatenate(scattered(part_kv), axis=0)

    def columns(first):
        return jnp.concatenate(
            [grad_w_kv[:, c : c + HD] for c in range(first, 2 * HD * kv_heads, 2 * HD)], axis=1
        )

    return (grad_x, grad_w_query, columns(0), columns(HD))


def solution(mesh):
    return jax.shard_map(
        shards,
        mesh=mesh,
        in_specs=(
            P("ctx", "tp"),
            P(None, "tp"),
            P(None, "tp"),
            P(None, "tp"),
            P("ctx", "tp"),
            P("ctx", "tp"),
            P("ctx", "tp"),
            P("ctx", "tp"),
            P("ctx", None),
            P(),
        ),
        out_specs=(P("ctx", "tp"), P("ctx", "tp"), P("ctx", "tp"), P("ctx", "tp")),
        check_vma=False,
    )
```

```python
import functools
import math

import jax
import jax.numpy as jnp
from jax import lax
from jax.experimental import pallas as pl
from jax.experimental.pallas import tpu as pltpu
from jax.sharding import PartitionSpec as P

H = 40
KVH = 8
HD = 128
BLK = 128
NGLOB = 2
GROUPS = H // KVH
ROWS = GROUPS * BLK
TURN = 8
SPAN = TURN * BLK
SCALE = 1.0 / math.sqrt(HD)
EXP_SCALE = SCALE * math.log2(math.e)
MASKED = -1e30
BF16 = jnp.bfloat16
F32 = jnp.float32
MIB = 1024 * 1024


def fold_rows(x):
    return x.reshape(x.shape[0] // 8, 8, x.shape[1])


def attn_kernel(places, tok_rows, lists, globs, here, q_ref, do_ref, *refs):
    pieces, refs = refs[: len(places)], refs[len(places) :]
    dq_ref, same_ref, other_ref, kv_ref, s_ref, dp_ref, dqt_ref, dk_acc, dv_acc, ids = refs
    step = pl.program_id(0)
    me = here[0]
    ctx_size = kv_ref.shape[0] // tok_rows

    @pl.when(step == 0)
    def _():
        dk_acc[...] = jnp.zeros_like(dk_acc)
        dv_acc[...] = jnp.zeros_like(dv_acc)
        for mask, piece in zip(places, pieces):
            start = pl.multiple_of((me ^ mask) * tok_rows, BLK)
            kv_ref[pl.ds(start, piece.shape[0]), :] = piece[...]

    blk = me * (tok_rows // BLK) + step
    is_global = globs[0] == blk
    for g in range(1, NGLOB):
        is_global = is_global | (globs[g] == blk)

    def all_before():
        def put(i, carry):
            ids[TURN + i] = i
            return carry

        lax.fori_loop(0, blk, put, 0)
        return blk

    def listed():
        count = jnp.int32(0)
        for slot in range(lists.shape[1]):
            other = lists[step, slot]
            ids[TURN + count] = jnp.maximum(other, 0)
            count = count + jnp.where((other >= 0) & (other != blk), 1, 0)
        for g in range(NGLOB):
            other = globs[g]
            ids[TURN + count] = other
            count = count + jnp.where(other <= blk, 1, 0)
        return count

    count = lax.cond(is_global, all_before, listed)
    extra = lax.rem(count, TURN)
    ids[0] = blk
    for i in range(1, TURN):
        ids[i] = jnp.where(i <= extra, ids[jnp.maximum(TURN + count - i, 0)], blk)
    turns = 1 + lax.div(count, TURN)

    def stacked(ref):
        return jnp.concatenate([ref[:, g * HD : (g + 1) * HD] for g in range(GROUPS)], axis=0)

    q_rows = stacked(q_ref)
    do_rows = stacked(do_ref)
    q_cols = q_rows.T
    do_cols = do_rows.T

    def start_of(i):
        return pl.multiple_of(ids[i] * BLK, BLK)

    def keys_of(p, half):
        cols = slice(half * HD, (half + 1) * HD)
        return jnp.concatenate(
            [kv_ref[pl.ds(start_of(TURN * p + i), BLK), cols] for i in range(TURN)], axis=0
        )

    def at(p):
        return pl.ds(pl.multiple_of(p * SPAN, SPAN), SPAN)

    def scores_of(p):
        return jnp.dot(keys_of(p, 0), q_cols, preferred_element_type=F32)

    key_pos = lax.broadcasted_iota(jnp.int32, (BLK, ROWS), 0)
    query_pos = lax.broadcasted_iota(jnp.int32, (BLK, ROWS), 1) & (BLK - 1)
    scores = scores_of(0)
    parts = [jnp.where(key_pos <= query_pos, scores[:BLK], MASKED)]
    for i in range(1, TURN):
        bias = jnp.where(i <= extra, 0.0, MASKED).astype(F32)
        parts.append(scores[i * BLK : (i + 1) * BLK] + bias)
    scores = jnp.concatenate(parts, axis=0)
    s_ref[at(0), :] = scores
    top8 = jnp.max(fold_rows(scores), axis=0)

    def score_pass(p, top8):
        scores = scores_of(p)
        s_ref[at(p), :] = scores
        return jnp.maximum(top8, jnp.max(fold_rows(scores), axis=0))

    top8 = lax.fori_loop(1, turns, score_pass, top8)
    top = jnp.max(top8, axis=0, keepdims=True)

    def sum_pass(p, carry):
        total8, dot8 = carry
        e = jnp.exp2((s_ref[at(p), :] - top) * EXP_SCALE)
        dp = jnp.dot(keys_of(p, 1), do_cols, preferred_element_type=F32)
        s_ref[at(p), :] = e
        dp_ref[at(p), :] = dp
        return (
            total8 + jnp.sum(fold_rows(e), axis=0),
            dot8 + jnp.sum(fold_rows(e * dp), axis=0),
        )

    zero8 = jnp.zeros((8, ROWS), F32)
    total8, dot8 = lax.fori_loop(0, turns, sum_pass, (zero8, zero8))
    inverse = 1.0 / jnp.sum(total8, axis=0, keepdims=True)
    delta = jnp.sum(dot8, axis=0, keepdims=True) * inverse
    dqt_ref[...] = jnp.zeros_like(dqt_ref)

    def grad_pass(p, carry):
        prob = s_ref[at(p), :] * inverse
        ds = (prob * (dp_ref[at(p), :] - delta)).astype(BF16)
        dv = jnp.dot(prob.astype(BF16), do_rows, preferred_element_type=F32)
        dk = jnp.dot(ds, q_rows, preferred_element_type=F32)
        dqt_ref[...] += jnp.dot(keys_of(p, 0).T, ds, preferred_element_type=F32)
        for i in range(TURN):
            rows = pl.ds(start_of(TURN * p + i), BLK)
            part = slice(i * BLK, (i + 1) * BLK)
            dk_acc[rows, :] += dk[part]
            dv_acc[rows, :] += dv[part]
        return carry

    lax.fori_loop(0, turns, grad_pass, 0)
    dq = (dqt_ref[...] * SCALE).T.astype(BF16)
    for g in range(GROUPS):
        dq_ref[:, g * HD : (g + 1) * HD] = dq[g * BLK : (g + 1) * BLK]

    @pl.when(step == pl.num_programs(0) - 1)
    def _():
        for chip in range(ctx_size // 2):
            out = slice(chip * tok_rows, (chip + 1) * tok_rows)
            for ref, core in ((same_ref, 0), (other_ref, 1)):
                start = pl.multiple_of((me ^ (2 * chip + core)) * tok_rows, BLK)
                rows = pl.ds(start, tok_rows)
                ref[out, :HD] = (dk_acc[rows, :] * SCALE).astype(BF16)
                ref[out, HD:] = dv_acc[rows, :].astype(BF16)


def attention_grads(head, block_lists, global_ids, here, queries, grad_out, places, pieces):
    tok_rows = queries.shape[0]
    blk_count = tok_rows // BLK
    total_rows = sum(piece.shape[0] for piece in pieces)
    slots = max(block_lists.shape[1] + NGLOB + 1, total_rows // BLK // 2)
    slots = -(-slots // TURN) * TURN
    smem = pl.BlockSpec(memory_space=pltpu.SMEM)
    pair_cols = 2 * HD
    work = blk_count * 9 * BLK * ROWS
    half = pl.BlockSpec((total_rows // 2, pair_cols), lambda a: (0, 0))
    half_shape = jax.ShapeDtypeStruct((total_rows // 2, pair_cols), BF16)
    return pl.pallas_call(
        functools.partial(attn_kernel, places, tok_rows),
        grid=(blk_count,),
        in_specs=[
            smem,
            smem,
            smem,
            pl.BlockSpec((BLK, ROWS), lambda a: (a, head)),
            pl.BlockSpec((BLK, ROWS), lambda a: (a, head)),
        ]
        + [
            pl.BlockSpec(piece.shape, lambda a: (0, 0), pipeline_mode=pl.Buffered(1))
            for piece in pieces
        ],
        out_specs=[pl.BlockSpec((BLK, ROWS), lambda a: (a, 0)), half, half],
        out_shape=[jax.ShapeDtypeStruct((tok_rows, ROWS), BF16), half_shape, half_shape],
        scratch_shapes=[
            pltpu.VMEM((total_rows, pair_cols), BF16),
            pltpu.VMEM((slots * BLK, ROWS), F32),
            pltpu.VMEM((slots * BLK, ROWS), F32),
            pltpu.VMEM((HD, ROWS), F32),
            pltpu.VMEM((total_rows, HD), F32),
            pltpu.VMEM((total_rows, HD), F32),
            pltpu.SMEM((slots + TURN + 1,), jnp.int32),
        ],
        compiler_params=pltpu.CompilerParams(
            dimension_semantics=("arbitrary",), vmem_limit_bytes=58 * MIB
        ),
        cost_estimate=pl.CostEstimate(flops=1000, transcendentals=0, bytes_accessed=1000),
        name="attn_grads",
    )(block_lists, global_ids, here, queries, grad_out, *pieces)


def dot_t(rows, weight):
    return lax.dot_general(rows, weight, (((1,), (1,)), ((), ())), preferred_element_type=F32)


def query_term_kernel(heads, *refs):
    dq, (wq_ref, out_ref) = refs[:heads], refs[heads:]
    total = dot_t(dq[0][...], wq_ref[:, :ROWS])
    for j in range(1, heads):
        total += dot_t(dq[j][...], wq_ref[:, j * ROWS : (j + 1) * ROWS])
    out_ref[...] = total.astype(BF16)


def query_term(dq, w_query):
    rows, (width, cols) = dq[0].shape[0], w_query.shape
    tile = width // 4
    return pl.pallas_call(
        functools.partial(query_term_kernel, len(dq)),
        grid=(width // tile,),
        in_specs=[pl.BlockSpec(x.shape, lambda i: (0, 0)) for x in dq]
        + [pl.BlockSpec((tile, cols), lambda i: (i, 0))],
        out_specs=pl.BlockSpec((rows, tile), lambda i: (0, i)),
        out_shape=jax.ShapeDtypeStruct((rows, width), BF16),
        compiler_params=pltpu.CompilerParams(
            dimension_semantics=("arbitrary",), vmem_limit_bytes=58 * MIB
        ),
        cost_estimate=pl.CostEstimate(flops=1000, transcendentals=0, bytes_accessed=1000),
        name="query_term",
    )(*dq, w_query)


def kv_term_kernel(heads, *refs):
    grads, (base_ref, wk_ref, wv_ref, out_ref, dk_ref, dv_ref) = refs[:heads], refs[heads:]

    @pl.when(pl.program_id(0) == 0)
    def _():
        for j in range(heads):
            cols = slice(j * HD, (j + 1) * HD)
            dk_ref[:, cols] = grads[j][:, :HD]
            dv_ref[:, cols] = grads[j][:, HD:]

    total = base_ref[...].astype(F32) + dot_t(dk_ref[...], wk_ref[...]) + dot_t(dv_ref[...], wv_ref[...])
    out_ref[...] = total.astype(BF16)


def with_kv_term(base, dkv, w_key, w_value):
    rows, width = base.shape
    cols = w_key.shape[1]
    tile = width // 4
    weight = pl.BlockSpec((tile, cols), lambda i: (i, 0))
    return pl.pallas_call(
        functools.partial(kv_term_kernel, len(dkv)),
        grid=(width // tile,),
        in_specs=[pl.BlockSpec(x.shape, lambda i: (0, 0)) for x in dkv]
        + [pl.BlockSpec((rows, tile), lambda i: (0, i)), weight, weight],
        out_specs=pl.BlockSpec((rows, tile), lambda i: (0, i)),
        out_shape=jax.ShapeDtypeStruct((rows, width), BF16),
        scratch_shapes=[pltpu.VMEM((rows, cols), BF16)] * 2,
        compiler_params=pltpu.CompilerParams(
            dimension_semantics=("arbitrary",), vmem_limit_bytes=58 * MIB
        ),
        cost_estimate=pl.CostEstimate(flops=1000, transcendentals=0, bytes_accessed=1000),
        name="kv_term",
    )(*dkv, base, w_key, w_value)


def weight_grad_kernel(count, chip, x_ref, *refs):
    out_ref = refs[-1]
    own, partner = refs[:count], refs[count : 2 * count]
    inputs = x_ref[0].T
    rows = own[0].shape[0]
    start = 0
    for mine, theirs in zip(own, partner):
        total = jnp.dot(inputs[:, :rows], mine[...], preferred_element_type=F32)
        total += jnp.dot(inputs[:, rows:], theirs[...], preferred_element_type=F32)
        cols = mine.shape[1]
        out_ref[0, :, start : start + cols] = total.astype(BF16)
        start += cols


def weight_grad(chip, inputs, own, partner):
    chips, rows, width = inputs.shape
    cols = sum(x.shape[1] for x in own)
    return pl.pallas_call(
        functools.partial(weight_grad_kernel, len(own)),
        grid_spec=pltpu.PrefetchScalarGridSpec(
            num_scalar_prefetch=1,
            grid=(chips,),
            in_specs=[pl.BlockSpec((1, rows, width), lambda i, chip: (chip[0] ^ i, 0, 0))]
            + [pl.BlockSpec(x.shape, lambda i, chip: (0, 0)) for x in own + partner],
            out_specs=pl.BlockSpec((1, width, cols), lambda i, chip: (i, 0, 0)),
        ),
        out_shape=jax.ShapeDtypeStruct((chips, width, cols), BF16),
        compiler_params=pltpu.CompilerParams(
            dimension_semantics=("arbitrary",), vmem_limit_bytes=58 * MIB
        ),
        cost_estimate=pl.CostEstimate(flops=1000, transcendentals=0, bytes_accessed=1000),
        name="weight_grad",
    )(chip, inputs, *own, *partner)


def swap(x, mask):
    return lax.ppermute(x, "ctx", [(i, i ^ mask) for i in range(lax.axis_size("ctx"))])


def gather_pieces(x):
    size = lax.axis_size("ctx")
    found = [(0, x)] + [(mask, swap(x, mask)) for mask in range(2, size, 2)]
    return found + [(mask ^ 1, swap(piece, 1)) for mask, piece in found]


def after(x, *others):
    return lax.optimization_barrier((x, others))[0]


def total_of(parts):
    total = parts[0].astype(F32)
    for part in parts[1:]:
        total = total + part.astype(F32)
    return total.astype(BF16)


def scattered(partial):
    chips, rows, _ = partial.shape
    if chips != 4:
        top = total_of([partial[0]] + [swap(partial[i], 2 * i) for i in range(1, chips)])
        return [top]
    half = rows // 2
    by_side, by_front = swap(partial[3, :half], 2), swap(partial[3, half:], 4)
    side_top, front_low = swap(partial[1, :half], 2), swap(partial[2, half:], 4)
    front_top = swap(total_of([partial[2, :half], by_side]), 4)
    side_low = swap(total_of([partial[1, half:], by_front]), 2)
    return [
        total_of([partial[0, :half], side_top, front_top]),
        total_of([partial[0, half:], side_low, front_low]),
    ]


def shards(
    layer_input, w_query, w_key, w_value, queries, keys, values, grad_out, block_lists, global_ids
):
    tok_rows, width = layer_input.shape
    kv_heads = keys.shape[1] // HD
    chips = lax.axis_size("ctx") // 2
    here = lax.axis_index("ctx").astype(jnp.int32)
    core = here & 1
    chip = (here >> 1).reshape(1)

    def own_kv(j):
        cols = slice(j * HD, (j + 1) * HD)
        return jnp.concatenate([keys[:, cols], values[:, cols]], axis=1)

    size = lax.axis_size("ctx")
    gathered = [gather_pieces(own_kv(0))]
    arrived = [piece for _, piece in gathered[0]]
    for j in range(1, kv_heads):
        own = after(own_kv(j), *arrived)
        gathered.append([(0, own)] + [(mask, swap(own, mask)) for mask in range(2, size, 2)])

    half = width // 2
    kept, given = (
        lax.dynamic_slice(
            layer_input, (0, start * half), (tok_rows, half), allow_negative_indices=False
        )
        for start in (core, 1 - core)
    )
    input_pair = jnp.concatenate([kept, swap(given, 1)], axis=0)
    inputs = lax.all_gather(input_pair, "tp", axis=0, tiled=False)

    dq, dkv = [], []
    ready = ()
    for j in range(kv_heads):
        dq_j, same, other = attention_grads(
            j,
            block_lists,
            global_ids,
            after(here.reshape(1), *ready),
            queries,
            grad_out,
            [mask for mask, _ in gathered[j]],
            [piece for _, piece in gathered[j]],
        )
        dq.append(dq_j)
        if j + 1 < kv_heads:
            early = [(mask, after(piece, dq_j)) for mask, piece in gathered[j + 1]]
            other = after(other, *[piece for _, piece in early])
            gathered[j + 1] = early + [(mask ^ 1, swap(piece, 1)) for mask, piece in early]
        other = after(other, *dkv)
        chip_sum = total_of([same, swap(other, 1)]).reshape(chips, tok_rows, 2 * HD)
        ready = (chip_sum,)
        if j == kv_heads - 1:
            dq_partner = [swap(x, 1) for x in dq]
            base = query_term(
                [after(dq[0], chip_sum, *dq_partner)] + dq[1:], w_query
            )
            chip_sum_last = after(chip_sum[0], base)
        else:
            chip_sum_last = after(chip_sum[0], *dq)
        dkv.append(
            total_of([chip_sum_last] + [swap(chip_sum[i], 2 * i) for i in range(1, chips)])
        )
    input_term = with_kv_term(base, dkv, w_key, w_value)
    grad_x = lax.psum_scatter(input_term, "tp", scatter_dimension=1, tiled=True)
    dkv_partner = [swap(x, 1) for x in dkv]

    part_query = weight_grad(
        chip, after(inputs, input_term), dq, dq_partner
    )
    part_kv = weight_grad(chip, inputs, [after(dkv[0], part_query)] + dkv[1:], dkv_partner)
    grad_w_query = jnp.concatenate(scattered(part_query), axis=0)
    grad_w_kv = jnp.concatenate(scattered(part_kv), axis=0)

    def columns(first):
        return jnp.concatenate(
            [grad_w_kv[:, c : c + HD] for c in range(first, 2 * HD * kv_heads, 2 * HD)], axis=1
        )

    return (grad_x, grad_w_query, columns(0), columns(HD))


def solution(mesh):
    return jax.shard_map(
        shards,
        mesh=mesh,
        in_specs=(
            P("ctx", "tp"),
            P(None, "tp"),
            P(None, "tp"),
            P(None, "tp"),
            P("ctx", "tp"),
            P("ctx", "tp"),
            P("ctx", "tp"),
            P("ctx", "tp"),
            P("ctx", None),
            P(),
        ),
        out_specs=(P("ctx", "tp"), P("ctx", "tp"), P("ctx", "tp"), P("ctx", "tp")),
        check_vma=False,
    )
```
